128 devices in a mesh: segment: 4 (over y_lo, core), slab: 32 (over z, x, y_hi).
Axes of the slice: x: 4, y: 4 (y_hi: 2, y_lo: 2; y = y_hi * 2 + y_lo), z: 4, core: 2. Of those that a mesh axis runs over, the one named last changes fastest.
Arguments:
- video_in: bfloat16 [8, 64, 64, 384], P(None, 'slab'), may hold values from -6 to 6
- cache_in: bfloat16 [4, 2, 64, 64, 384], P('segment', None, 'slab'), may hold values from -0.25 to 2
- conv_weight: bfloat16 [4, 3, 3, 3, 384, 384], P('segment'), may hold values from -0.0625 to 0.0625
- conv_bias: float32 [4, 384], P('segment'), may hold values from -1.5 to 1.5
- norm_gain: float32 [4, 384], P('segment'), may hold values from 0.5 to 2
Outputs:
- video_out: bfloat16 [8, 64, 64, 384], P('segment', 'slab')
- cache_out: bfloat16 [4, 2, 64, 64, 384], P('segment', None, 'slab')
The draws below stay inside these ranges and needn't reach their ends.
All inputs are finite; a program needn't handle non-finite values.
Results may differ from the reference program's by a relative error of at most 0.0067.
Values may be sent and summed in bfloat16 or wider, within the bound.
A program may use at most 64 MiB of HBM per device.

```python
import math
import jax
import jax.numpy as jnp
from jax import lax

CHANNELS = 384
COLUMNS = 64
LAYERS = 4
FRAMES = 8
HEIGHT = 64


def block_levels(own_key, dims, cuts, least, top_value):
    factor_of, own = 1.0, jax.random.fold_in(own_key, 6)
    for axis_at, blocks in cuts:
        draws = jnp.exp(jax.random.uniform(jax.random.fold_in(own, axis_at), (blocks,), jnp.float32, least / len(cuts), top_value / len(cuts)))
        factor_of = factor_of * jnp.repeat(draws, dims[axis_at] // blocks).reshape([-1 if axis == axis_at else 1 for axis in range(len(dims))])
    return factor_of


def centred(rng, shape, width, limit, shards=(), held_as=jnp.bfloat16):
    factor_of = block_levels(rng, shape, shards, -0.22, 0.18) if shards else 1.0
    entries = jax.random.normal(rng, shape, jnp.float32) * width * factor_of
    return jnp.minimum(jnp.maximum(entries, -limit), limit).astype(held_as)


def setup_inputs(seed: int = 0) -> dict:
    key_of = jax.random.split(jax.random.key(seed), 6)
    video_in = centred(key_of[0], (FRAMES, HEIGHT, COLUMNS, CHANNELS), 1.0, 6.0, ((1, 32),))
    cache_in = jnp.clip(-0.25 + 2.25 * jax.random.uniform(key_of[1], (LAYERS, 2, HEIGHT, COLUMNS, CHANNELS), jnp.float32) ** block_levels(key_of[1], (LAYERS, 2, HEIGHT, COLUMNS, CHANNELS), ((0, 4), (2, 32)), -0.2, 0.2), -0.25, 2.0).astype(jnp.bfloat16)
    conv_weight = centred(key_of[2], (LAYERS, 3, 3, 3, CHANNELS, CHANNELS), (27 * CHANNELS) ** -0.5, 0.0625, ((0, 4),))
    conv_bias = centred(key_of[3], (LAYERS, CHANNELS), 0.3, 1.5, ((0, 4),), jnp.float32)
    norm_gain = jnp.clip(jnp.exp(math.log(2.0) - 1.3862944 * jax.random.uniform(key_of[4], (LAYERS, CHANNELS), jnp.float32) ** block_levels(key_of[4], (LAYERS, CHANNELS), ((0, 4),), -0.2, 0.2)), 0.5, 2.0)
    return {"video_in": video_in, "cache_in": cache_in, "conv_weight": conv_weight, "conv_bias": conv_bias, "norm_gain": norm_gain}


def activate(layer_in, gain):
    values = layer_in.astype(jnp.float32)
    scaled = values * lax.rsqrt(lax.optimization_barrier(jnp.mean(values * values, axis=-1, keepdims=True)) + 1e-06) * gain.astype(jnp.float32)
    return jax.nn.silu(scaled).astype(jnp.bfloat16)

def convolve(padded, weight, bias, frames_out):
    rows_out = padded.shape[1] - 2
    cols_out = padded.shape[2] - 2
    total = jnp.zeros((frames_out * rows_out * cols_out, CHANNELS), jnp.float32) + bias.astype(jnp.float32)
    for shift_t in range(3):
        for shift_h in range(3):
            for shift_w in range(3):
                piece = padded[shift_t:shift_t + frames_out, shift_h:shift_h + rows_out, shift_w:shift_w + cols_out]
                total = total + jnp.dot(piece.reshape(-1, CHANNELS), weight[shift_t, shift_h, shift_w], preferred_element_type=jnp.float32)
    return total.reshape(frames_out, rows_out, cols_out, CHANNELS)

def reference(video_in, cache_in, conv_weight, conv_bias, norm_gain):
    current = video_in
    caches = []
    for layer in range(LAYERS):
        acts = activate(current, norm_gain[layer])
        full = jnp.concatenate([cache_in[layer], acts], axis=0)
        padded = jnp.pad(full, ((0, 0), (1, 1), (1, 1), (0, 0)))
        conv = convolve(padded, conv_weight[layer], conv_bias[layer], FRAMES)
        current = (current.astype(jnp.float32) + conv).astype(jnp.bfloat16)
        caches.append(full[-2:])
    return (current, jnp.stack(caches))
```

```python
import jax
import jax.numpy as jnp
from jax import lax
from jax.experimental import pallas as pl
from jax.experimental.pallas import tpu as pltpu
from jax.sharding import PartitionSpec as P

MESH = pl.DeviceIdType.MESH
PITCH = 40


def kernel(video, cache, weight, bias, gain, vout, cout, wbuf, xin, cin, lhs, flat, acc, outb, actb,
           w_sem, loc_sem, in_sem, in_send, pipe_send, vin_send, cin_loc, cin_sem, cin_send, vo_send, vo_sem, co_send, co_sem):
    frames = video.shape[0]
    channels = video.shape[-1]
    rows = xin.shape[1]
    tall = rows - 2
    size = tall * PITCH
    span = rows * PITCH
    taps = weight.shape[1] // channels
    half = video.shape[2] // 2
    shift = video.shape[2] - PITCH
    lead = PITCH - half
    seg = lax.axis_index("segment")
    slab = lax.axis_index("slab")
    segs = lax.axis_size("segment")
    groups = lax.axis_size("slab") // 2
    last = segs - 1
    k = slab // 2
    hi = slab % 2
    first_seg = seg == 0
    top = k == 0
    bottom = k == groups - 1

    def at(s, kk, h):
        return (s, kk * 2 + h)

    def remote(src, dst, send, recv, dev):
        return pltpu.make_async_remote_copy(src_ref=src, dst_ref=dst, send_sem=send, recv_sem=recv, device_id=dev, device_id_type=MESH)

    def cols(h):
        return pl.ds(pl.multiple_of(h * shift, 8), PITCH)

    def own_cols(h):
        return pl.ds(pl.multiple_of(h * lead, 8), half)

    def out_cols(h):
        return pl.ds(pl.multiple_of(h * half, 8), half)

    third = weight.shape[1] // 3

    def w_copy(a, b):
        return pltpu.make_async_copy(weight.at[a, pl.ds(b * third, third), :], wbuf.at[pl.ds(b * third, third), pl.ds((2 - a) * channels, channels)], w_sem.at[a, b])

    def own_video(f):
        return pltpu.make_async_copy(video.at[f, :, cols(hi), :], xin.at[f, pl.ds(1 + 2 * hi, 2)], loc_sem.at[f])

    own_cache = pltpu.make_async_copy(cache.at[:, :, cols(hi), :], cin.at[:, pl.ds(1 + 2 * hi, 2)], cin_loc)

    own_cache.start()

    @pl.when(first_seg)
    def _():
        for f in range(frames):
            own_video(f).start()

    for a in (2, 1, 0):
        for b in range(3):
            w_copy(a, b).start()

    @pl.when(top)
    def _():
        xin[:, 0] = jnp.zeros_like(xin[:, 0])
        cin[:, 0] = jnp.zeros_like(cin[:, 0])

    @pl.when(bottom)
    def _():
        xin[:, rows - 1] = jnp.zeros_like(xin[:, rows - 1])
        cin[:, rows - 1] = jnp.zeros_like(cin[:, rows - 1])

    flat[0:8] = jnp.zeros((8, channels), jnp.float32)
    flat[8 + span:16 + span] = jnp.zeros((8, channels), jnp.float32)

    barrier = pltpu.get_barrier_semaphore()
    step_k = 2 * hi - 1
    inner = jnp.logical_and(k + step_k >= 0, k + step_k < groups)

    def greet(dev):
        pl.semaphore_signal(barrier, inc=1, device_id=dev, device_id_type=MESH)

    greet(at(seg, k, 1 - hi))
    pl.when(jnp.logical_not(top))(lambda: greet(at(seg, k - 1, 1)))
    pl.when(jnp.logical_not(bottom))(lambda: greet(at(seg, k + 1, 0)))

    @pl.when(seg > 0)
    def _():
        greet(at(seg - 1, k, hi))
        pl.when(jnp.logical_not(top))(lambda: greet(at(seg - 1, k - 1, hi)))
        pl.when(jnp.logical_not(bottom))(lambda: greet(at(seg - 1, k + 1, hi)))

    @pl.when(first_seg)
    def _():
        greet(at(2, k, 1 - hi))
        pl.when(jnp.logical_not(top))(lambda: greet(at(3 - 2 * hi, k - 1, 1)))
        pl.when(jnp.logical_not(bottom))(lambda: greet(at(1 + 2 * hi, k + 1, 0)))

    @pl.when(seg < last)
    def _():
        greet(at(last, k, 0))
        greet(at(last, k, 1))

    @pl.when(seg == last)
    def _():
        greet(at(last, k, 1 - hi))

    one = jnp.int32(1)
    zero = jnp.int32(0)
    edge_count = jnp.where(top, zero, one) + jnp.where(bottom, zero, one)
    inner_count = jnp.where(inner, one, zero)
    expected = 1 + 2 * inner_count
    expected += jnp.where(seg < last, 1 + edge_count, zero)
    expected += jnp.where(seg == 2, one, zero)
    expected += jnp.where(jnp.logical_or(seg == 1, seg == 3), inner_count, zero)
    expected += jnp.where(seg == last, 2 * last + 1, zero)
    pl.semaphore_wait(barrier, expected)

    def send_slab(f):
        return remote(video.at[f, :, cols(1 - hi), :], xin.at[f, pl.ds(1 + 2 * hi, 2)], vin_send.at[f], in_sem.at[f, 0], at(0, k, 1 - hi))

    edge_row = (rows - 1) * (1 - hi)
    edge_sem = 2 - hi

    def send_edge(f):
        to = jnp.where(seg == 1, hi, 1 - hi)
        return remote(video.at[f, hi, cols(to), :], xin.at[f, edge_row], vin_send.at[f], in_sem.at[f, edge_sem], at(0, k + step_k, to))

    def send_cache_slab():
        return remote(cache.at[:, :, cols(1 - hi), :], cin.at[:, pl.ds(1 + 2 * hi, 2)], cin_send.at[0], cin_sem.at[0], at(seg, k, 1 - hi))

    def send_cache_edge(h):
        return remote(cache.at[:, hi, cols(h), :], cin.at[:, edge_row], cin_send.at[1 + h], cin_sem.at[edge_sem], at(seg, k + step_k, h))

    @pl.when(seg == 2)
    def _():
        for f in range(frames):
            send_slab(f).start()

    @pl.when(jnp.logical_and(jnp.logical_or(seg == 1, seg == 3), inner))
    def _():
        for f in range(frames):
            send_edge(f).start()

    send_cache_slab().start()

    @pl.when(inner)
    def _():
        send_cache_edge(0).start()
        send_cache_edge(1).start()

    slot = lax.broadcasted_iota(jnp.int32, (rows, PITCH, channels), 1).reshape(span, channels)
    keep = slot != (PITCH - 1) * (1 - hi)

    def spread():
        for b in range(3):
            for c in range(3):
                start = 8 + b * PITCH + c - 1
                lhs[:, (b * 3 + c) * channels:(b * 3 + c + 1) * channels] = flat[start:start + size, :].astype(jnp.bfloat16)

    def wait_cache():
        own_cache.wait()
        remote(cache.at[:, :, cols(hi), :], cin.at[:, pl.ds(3 - 2 * hi, 2)], cin_send.at[0], cin_sem.at[0], at(seg, k, 1 - hi)).wait_recv()
        pl.when(jnp.logical_not(top))(lambda: remote(cache.at[:, 0, cols(hi), :], cin.at[:, 0], cin_send.at[1], cin_sem.at[1], at(seg, k, 1 - hi)).wait_recv())
        pl.when(jnp.logical_not(bottom))(lambda: remote(cache.at[:, 0, cols(hi), :], cin.at[:, rows - 1], cin_send.at[1], cin_sem.at[2], at(seg, k, 1 - hi)).wait_recv())

    def load_cache(j):
        values = cin[j].astype(jnp.float32).reshape(span, channels)
        flat[8:8 + span] = jnp.where(keep, values, 0.0)
        spread()

    for b in range(3):
        w_copy(0, b).wait()
        w_copy(1, b).wait()
        w_copy(2, b).wait()

    wait_cache()
    load_cache(1)
    later = jnp.dot(lhs[...], wbuf[:, channels:], preferred_element_type=jnp.float32)
    acc[0] = later[:, :channels]
    acc[1] = later[:, channels:]
    load_cache(0)
    acc[0] += jnp.dot(lhs[...], wbuf[:, 2 * channels:], preferred_element_type=jnp.float32)

    gains = gain[0:1, :]
    biases = bias[0:1, :]

    def pipe_own(f):
        return remote(outb.at[f], xin.at[f, pl.ds(1, tall)], pipe_send.at[f, 0], in_sem.at[f, 0], at(seg + 1, k, hi))

    def pipe_up(f):
        return remote(outb.at[f, 0], xin.at[f, rows - 1], pipe_send.at[f, 1], in_sem.at[f, 2], at(seg + 1, k - 1, hi))

    def pipe_down(f):
        return remote(outb.at[f, tall - 1], xin.at[f, 0], pipe_send.at[f, 2], in_sem.at[f, 1], at(seg + 1, k + 1, hi))

    per = frames // segs

    def vo_copy(f, h):
        return remote(outb.at[f, pl.ds(2 * h, 2), own_cols(hi), :], vout.at[f % per, :, out_cols(hi), :], vo_send.at[f, h], vo_sem.at[f % per, hi], at(f // per, k, h))

    def vo_local(f):
        return pltpu.make_async_copy(outb.at[f, pl.ds(2 * hi, 2), own_cols(hi), :], vout.at[f % per, :, out_cols(hi), :], vo_sem.at[f % per, hi])

    def co_copy(j):
        return remote(actb.at[j, pl.ds(2 * (1 - hi), 2), own_cols(hi), :], cout.at[j, :, out_cols(hi), :], co_send.at[j], co_sem.at[j, hi], at(seg, k, 1 - hi))

    def co_local(j):
        return pltpu.make_async_copy(actb.at[j, pl.ds(2 * hi, 2), own_cols(hi), :], cout.at[j, :, out_cols(hi), :], co_sem.at[j, hi])

    def frame(f, carry):
        @pl.when(first_seg)
        def _():
            own_video(f).wait()
            remote(video.at[f, :, cols(hi), :], xin.at[f, pl.ds(3 - 2 * hi, 2)], vin_send.at[f], in_sem.at[f, 0], at(1, k, hi)).wait_recv()

        @pl.when(seg > 0)
        def _():
            remote(outb.at[f], xin.at[f, pl.ds(1, tall)], vin_send.at[f], in_sem.at[f, 0], at(0, k, hi)).wait_recv()

        pl.when(jnp.logical_not(top))(lambda: remote(outb.at[f, 0], xin.at[f, 0], vin_send.at[f], in_sem.at[f, 1], at(0, k, 1 - hi)).wait_recv())
        pl.when(jnp.logical_not(bottom))(lambda: remote(outb.at[f, 0], xin.at[f, rows - 1], vin_send.at[f], in_sem.at[f, 2], at(0, k, 1 - hi)).wait_recv())

        values = xin[f].astype(jnp.float32).reshape(span, channels)
        mean = jnp.sum(values * values, axis=-1, keepdims=True) * (1.0 / channels)
        scaled = values * lax.rsqrt(mean + 1e-06) * gains
        acts = scaled / (1.0 + jnp.exp(-scaled))
        flat[8:8 + span] = jnp.where(keep, acts, 0.0)
        spread()

        @pl.when(f >= frames - 2)
        def _():
            j = f - (frames - 2)
            actb[j] = flat[8 + PITCH:8 + PITCH + size].reshape(tall, PITCH, channels).astype(jnp.bfloat16)
            co_copy(j).start()
            co_local(j).start()

        now = lax.rem(f, 3)
        conv = jnp.dot(lhs[...], wbuf[:, :channels], preferred_element_type=jnp.float32) + acc[now] + biases
        residual = xin[f, 1:1 + tall].astype(jnp.float32).reshape(size, channels)
        outb[f] = (residual + conv).reshape(tall, PITCH, channels).astype(jnp.bfloat16)

        @pl.when(seg < last)
        def _():
            pl.when(jnp.logical_not(top))(lambda: pipe_up(f).start())
            pl.when(jnp.logical_not(bottom))(lambda: pipe_down(f).start())
            pipe_own(f).start()

        @pl.when(seg == last)
        def _():
            @pl.when(f // per < last)
            def _():
                vo_copy(f, 0).start()
                vo_copy(f, 1).start()

            @pl.when(f // per == last)
            def _():
                vo_copy(f, 1 - hi).start()
                vo_local(f).start()

        @pl.when(f < frames - 1)
        def _():
            later = jnp.dot(lhs[...], wbuf[:, channels:], preferred_element_type=jnp.float32)
            nxt = lax.rem(f + 1, 3)
            acc[nxt] = acc[nxt] + later[:, :channels]
            acc[lax.rem(f + 2, 3)] = later[:, channels:]

        return carry

    lax.fori_loop(0, frames, frame, 0)

    for j in range(2):
        co_local(j).wait()
        co_copy(j).wait_send()
        remote(actb.at[j, pl.ds(0, 2), own_cols(hi), :], cout.at[j, :, out_cols(1 - hi), :], co_send.at[j], co_sem.at[j, 1 - hi], at(seg, k, 1 - hi)).wait_recv()

    def vo_recv(j, h):
        remote(outb.at[0, pl.ds(0, 2), own_cols(hi), :], vout.at[j, :, out_cols(h), :], vo_send.at[0, 0], vo_sem.at[j, h], at(seg, k, 1 - hi)).wait_recv()

    @pl.when(seg < last)
    def _():
        for j in range(per):
            vo_recv(j, 0)
            vo_recv(j, 1)

        def sent(f, carry):
            pipe_own(f).wait_send()
            pl.when(jnp.logical_not(top))(lambda: pipe_up(f).wait_send())
            pl.when(jnp.logical_not(bottom))(lambda: pipe_down(f).wait_send())
            return carry

        lax.fori_loop(0, frames, sent, 0)

    @pl.when(seg == last)
    def _():
        for f in range(frames):
            if f // per < last:
                vo_copy(f, 0).wait_send()
                vo_copy(f, 1).wait_send()
            else:
                vo_copy(f, 1 - hi).wait_send()
                vo_local(f).wait()
                vo_recv(f % per, 1 - hi)

    send_cache_slab().wait_send()

    @pl.when(inner)
    def _():
        send_cache_edge(0).wait_send()
        send_cache_edge(1).wait_send()

    @pl.when(seg == 2)
    def _():
        for f in range(frames):
            send_slab(f).wait_send()

    @pl.when(jnp.logical_and(jnp.logical_or(seg == 1, seg == 3), inner))
    def _():
        for f in range(frames):
            send_edge(f).wait_send()


def local(video_in, cache_in, conv_weight, conv_bias, norm_gain):
    frames, held, columns, channels = video_in.shape
    rows = 2 * held + 2
    tall = rows - 2
    size = tall * PITCH
    span = rows * PITCH
    weight = conv_weight.reshape(3, 9 * channels, channels)
    cache = cache_in[0]
    per = frames // lax.axis_size("segment")
    dma = pltpu.SemaphoreType.DMA
    video_out, cache_out = pl.pallas_call(
        kernel,
        out_shape=(
            jax.ShapeDtypeStruct((per, held, columns, channels), jnp.bfloat16),
            jax.ShapeDtypeStruct(cache.shape, jnp.bfloat16),
        ),
        in_specs=[pl.BlockSpec(memory_space=pl.ANY)] * 3 + [pl.BlockSpec(memory_space=pltpu.VMEM)] * 2,
        out_specs=(pl.BlockSpec(memory_space=pl.ANY), pl.BlockSpec(memory_space=pl.ANY)),
        scratch_shapes=[
            pltpu.VMEM((9 * channels, 3 * channels), jnp.bfloat16),
            pltpu.VMEM((frames, rows, PITCH, channels), jnp.bfloat16),
            pltpu.VMEM((2, rows, PITCH, channels), jnp.bfloat16),
            pltpu.VMEM((size, 9 * channels), jnp.bfloat16),
            pltpu.VMEM((span + 16, channels), jnp.float32),
            pltpu.VMEM((3, size, channels), jnp.float32),
            pltpu.VMEM((frames, tall, PITCH, channels), jnp.bfloat16),
            pltpu.VMEM((2, tall, PITCH, channels), jnp.bfloat16),
            dma((3, 3)), dma((frames,)), dma((frames, 3)), dma((1,)), dma((frames, 3)), dma((frames,)),
            dma, dma((3,)), dma((3,)), dma((frames, 2)), dma((per, 2)), dma((2,)), dma((2, 2)),
        ],
        compiler_params=pltpu.CompilerParams(collective_id=0, has_side_effects=True, vmem_limit_bytes=60 * 2**20),
    )(video_in, cache, weight, conv_bias, norm_gain)
    return video_out, cache_out[None]


def solution(mesh):
    return jax.shard_map(
        local,
        mesh=mesh,
        in_specs=(
            P(None, "slab", None, None),
            P("segment", None, "slab", None, None),
            P("segment", None, None, None, None, None),
            P("segment", None),
            P("segment", None),
        ),
        out_specs=(P("segment", "slab", None, None), P("segment", None, "slab", None, None)),
        check_vma=False,
    )
```

```python
import jax
import jax.numpy as jnp
from jax import lax
from jax.experimental import pallas as pl
from jax.experimental.pallas import tpu as pltpu
from jax.sharding import PartitionSpec as P

MESH = pl.DeviceIdType.MESH
PITCH = 64


def kernel(video, cache, weight, bias, gain, vout, cout, wbuf, xin, cin, lhs, flat, acc, outb, actb,
           w_sem, loc_sem, in_sem, in_send, pipe_send, vin_send, cin_loc, cin_sem, cin_send, vo_send, vo_sem, co_send, co_sem):
    frames = video.shape[0]
    channels = video.shape[-1]
    rows = xin.shape[1]
    tall = rows - 2
    size = tall * PITCH
    span = rows * PITCH
    taps = weight.shape[1] // channels
    half = video.shape[2] // 2
    shift = video.shape[2] - PITCH
    lead = PITCH - half
    seg = lax.axis_index("segment")
    slab = lax.axis_index("slab")
    segs = lax.axis_size("segment")
    groups = lax.axis_size("slab") // 2
    last = segs - 1
    k = slab // 2
    hi = slab % 2
    first_seg = seg == 0
    top = k == 0
    bottom = k == groups - 1

    def at(s, kk, h):
        return (s, kk * 2 + h)

    def remote(src, dst, send, recv, dev):
        return pltpu.make_async_remote_copy(src_ref=src, dst_ref=dst, send_sem=send, recv_sem=recv, device_id=dev, device_id_type=MESH)

    def cols(h):
        return pl.ds(pl.multiple_of(h * shift, 8), PITCH)

    def own_cols(h):
        return pl.ds(pl.multiple_of(h * lead, 8), half)

    def out_cols(h):
        return pl.ds(pl.multiple_of(h * half, 8), half)

    third = weight.shape[1] // 3

    def w_copy(a, b):
        return pltpu.make_async_copy(weight.at[a, pl.ds(b * third, third), :], wbuf.at[pl.ds(b * third, third), pl.ds((2 - a) * channels, channels)], w_sem.at[a, b])

    def own_video(f):
        return pltpu.make_async_copy(video.at[f, :, cols(hi), :], xin.at[f, pl.ds(1 + 2 * hi, 2)], loc_sem.at[f])

    own_cache = pltpu.make_async_copy(cache.at[:, :, cols(hi), :], cin.at[:, pl.ds(1 + 2 * hi, 2)], cin_loc)

    own_cache.start()

    @pl.when(first_seg)
    def _():
        for f in range(frames):
            own_video(f).start()

    for a in (2, 1, 0):
        for b in range(3):
            w_copy(a, b).start()

    @pl.when(top)
    def _():
        xin[:, 0] = jnp.zeros_like(xin[:, 0])
        cin[:, 0] = jnp.zeros_like(cin[:, 0])

    @pl.when(bottom)
    def _():
        xin[:, rows - 1] = jnp.zeros_like(xin[:, rows - 1])
        cin[:, rows - 1] = jnp.zeros_like(cin[:, rows - 1])

    flat[0:8] = jnp.zeros((8, channels), jnp.float32)
    flat[8 + span:16 + span] = jnp.zeros((8, channels), jnp.float32)

    barrier = pltpu.get_barrier_semaphore()
    step_k = 2 * hi - 1
    inner = jnp.logical_and(k + step_k >= 0, k + step_k < groups)

    def greet(dev):
        pl.semaphore_signal(barrier, inc=1, device_id=dev, device_id_type=MESH)

    greet(at(seg, k, 1 - hi))
    pl.when(jnp.logical_not(top))(lambda: greet(at(seg, k - 1, 1)))
    pl.when(jnp.logical_not(bottom))(lambda: greet(at(seg, k + 1, 0)))

    @pl.when(seg > 0)
    def _():
        greet(at(seg - 1, k, hi))
        pl.when(jnp.logical_not(top))(lambda: greet(at(seg - 1, k - 1, hi)))
        pl.when(jnp.logical_not(bottom))(lambda: greet(at(seg - 1, k + 1, hi)))

    @pl.when(first_seg)
    def _():
        greet(at(2, k, 1 - hi))
        pl.when(jnp.logical_not(top))(lambda: greet(at(3 - 2 * hi, k - 1, 1)))
        pl.when(jnp.logical_not(bottom))(lambda: greet(at(1 + 2 * hi, k + 1, 0)))

    @pl.when(seg < last)
    def _():
        greet(at(last, k, 0))
        greet(at(last, k, 1))

    @pl.when(seg == last)
    def _():
        greet(at(last, k, 1 - hi))

    one = jnp.int32(1)
    zero = jnp.int32(0)
    edge_count = jnp.where(top, zero, one) + jnp.where(bottom, zero, one)
    inner_count = jnp.where(inner, one, zero)
    expected = 1 + 2 * inner_count
    expected += jnp.where(seg < last, 1 + edge_count, zero)
    expected += jnp.where(seg == 2, one, zero)
    expected += jnp.where(jnp.logical_or(seg == 1, seg == 3), inner_count, zero)
    expected += jnp.where(seg == last, 2 * last + 1, zero)
    pl.semaphore_wait(barrier, expected)

    def send_slab(f):
        return remote(video.at[f, :, cols(1 - hi), :], xin.at[f, pl.ds(1 + 2 * hi, 2)], vin_send.at[f], in_sem.at[f, 0], at(0, k, 1 - hi))

    edge_row = (rows - 1) * (1 - hi)
    edge_sem = 2 - hi

    def send_edge(f):
        to = jnp.where(seg == 1, hi, 1 - hi)
        return remote(video.at[f, hi, cols(to), :], xin.at[f, edge_row], vin_send.at[f], in_sem.at[f, edge_sem], at(0, k + step_k, to))

    def send_cache_slab():
        return remote(cache.at[:, :, cols(1 - hi), :], cin.at[:, pl.ds(1 + 2 * hi, 2)], cin_send.at[0], cin_sem.at[0], at(seg, k, 1 - hi))

    def send_cache_edge(h):
        return remote(cache.at[:, hi, cols(h), :], cin.at[:, edge_row], cin_send.at[1 + h], cin_sem.at[edge_sem], at(seg, k + step_k, h))

    @pl.when(seg == 2)
    def _():
        for f in range(frames):
            send_slab(f).start()

    @pl.when(jnp.logical_and(jnp.logical_or(seg == 1, seg == 3), inner))
    def _():
        for f in range(frames):
            send_edge(f).start()

    send_cache_slab().start()

    @pl.when(inner)
    def _():
        send_cache_edge(0).start()
        send_cache_edge(1).start()

    slot = lax.broadcasted_iota(jnp.int32, (rows, PITCH, channels), 1).reshape(span, channels)
    keep = slot != (PITCH - 1) * (1 - hi)

    def spread():
        for b in range(3):
            for c in range(3):
                start = 8 + b * PITCH + c - 1
                lhs[:, (b * 3 + c) * channels:(b * 3 + c + 1) * channels] = flat[start:start + size, :].astype(jnp.bfloat16)

    def wait_cache():
        own_cache.wait()
        remote(cache.at[:, :, cols(hi), :], cin.at[:, pl.ds(3 - 2 * hi, 2)], cin_send.at[0], cin_sem.at[0], at(seg, k, 1 - hi)).wait_recv()
        pl.when(jnp.logical_not(top))(lambda: remote(cache.at[:, 0, cols(hi), :], cin.at[:, 0], cin_send.at[1], cin_sem.at[1], at(seg, k, 1 - hi)).wait_recv())
        pl.when(jnp.logical_not(bottom))(lambda: remote(cache.at[:, 0, cols(hi), :], cin.at[:, rows - 1], cin_send.at[1], cin_sem.at[2], at(seg, k, 1 - hi)).wait_recv())

    def load_cache(j):
        values = cin[j].astype(jnp.float32).reshape(span, channels)
        flat[8:8 + span] = jnp.where(keep, values, 0.0)
        spread()

    for b in range(3):
        w_copy(0, b).wait()
        w_copy(1, b).wait()
        w_copy(2, b).wait()

    wait_cache()
    load_cache(1)
    later = jnp.dot(lhs[...], wbuf[:, channels:], preferred_element_type=jnp.float32)
    acc[0] = later[:, :channels]
    acc[1] = later[:, channels:]
    load_cache(0)
    acc[0] += jnp.dot(lhs[...], wbuf[:, 2 * channels:], preferred_element_type=jnp.float32)

    gains = gain[0:1, :]
    biases = bias[0:1, :]

    def pipe_own(f):
        return remote(outb.at[f], xin.at[f, pl.ds(1, tall)], pipe_send.at[f, 0], in_sem.at[f, 0], at(seg + 1, k, hi))

    def pipe_up(f):
        return remote(outb.at[f, 0], xin.at[f, rows - 1], pipe_send.at[f, 1], in_sem.at[f, 2], at(seg + 1, k - 1, hi))

    def pipe_down(f):
        return remote(outb.at[f, tall - 1], xin.at[f, 0], pipe_send.at[f, 2], in_sem.at[f, 1], at(seg + 1, k + 1, hi))

    per = frames // segs

    def vo_copy(f, h):
        return remote(outb.at[f, pl.ds(2 * h, 2), own_cols(hi), :], vout.at[f % per, :, out_cols(hi), :], vo_send.at[f, h], vo_sem.at[f % per, hi], at(f // per, k, h))

    def vo_local(f):
        return pltpu.make_async_copy(outb.at[f, pl.ds(2 * hi, 2), own_cols(hi), :], vout.at[f % per, :, out_cols(hi), :], vo_sem.at[f % per, hi])

    def co_copy(j):
        return remote(actb.at[j, pl.ds(2 * (1 - hi), 2), own_cols(hi), :], cout.at[j, :, out_cols(hi), :], co_send.at[j], co_sem.at[j, hi], at(seg, k, 1 - hi))

    def co_local(j):
        return pltpu.make_async_copy(actb.at[j, pl.ds(2 * hi, 2), own_cols(hi), :], cout.at[j, :, out_cols(hi), :], co_sem.at[j, hi])

    def frame(f, carry):
        @pl.when(first_seg)
        def _():
            own_video(f).wait()
            remote(video.at[f, :, cols(hi), :], xin.at[f, pl.ds(3 - 2 * hi, 2)], vin_send.at[f], in_sem.at[f, 0], at(1, k, hi)).wait_recv()

        @pl.when(seg > 0)
        def _():
            remote(outb.at[f], xin.at[f, pl.ds(1, tall)], vin_send.at[f], in_sem.at[f, 0], at(0, k, hi)).wait_recv()

        pl.when(jnp.logical_not(top))(lambda: remote(outb.at[f, 0], xin.at[f, 0], vin_send.at[f], in_sem.at[f, 1], at(0, k, 1 - hi)).wait_recv())
        pl.when(jnp.logical_not(bottom))(lambda: remote(outb.at[f, 0], xin.at[f, rows - 1], vin_send.at[f], in_sem.at[f, 2], at(0, k, 1 - hi)).wait_recv())

        values = xin[f].astype(jnp.float32).reshape(span, channels)
        mean = jnp.sum(values * values, axis=-1, keepdims=True) * (1.0 / channels)
        scaled = values * lax.rsqrt(mean + 1e-06) * gains
        acts = scaled / (1.0 + jnp.exp(-scaled))
        flat[8:8 + span] = jnp.where(keep, acts, 0.0)
        spread()

        @pl.when(f >= frames - 2)
        def _():
            j = f - (frames - 2)
            actb[j] = flat[8 + PITCH:8 + PITCH + size].reshape(tall, PITCH, channels).astype(jnp.bfloat16)
            co_copy(j).start()
            co_local(j).start()

        now = lax.rem(f, 3)
        conv = jnp.dot(lhs[...], wbuf[:, :channels], preferred_element_type=jnp.float32) + acc[now] + biases
        residual = xin[f, 1:1 + tall].astype(jnp.float32).reshape(size, channels)
        outb[f] = (residual + conv).reshape(tall, PITCH, channels).astype(jnp.bfloat16)

        @pl.when(seg < last)
        def _():
            pl.when(jnp.logical_not(top))(lambda: pipe_up(f).start())
            pl.when(jnp.logical_not(bottom))(lambda: pipe_down(f).start())
            pipe_own(f).start()

        @pl.when(seg == last)
        def _():
            @pl.when(f // per < last)
            def _():
                vo_copy(f, 0).start()
                vo_copy(f, 1).start()

            @pl.when(f // per == last)
            def _():
                vo_copy(f, 1 - hi).start()
                vo_local(f).start()

        @pl.when(f < frames - 1)
        def _():
            later = jnp.dot(lhs[...], wbuf[:, channels:], preferred_element_type=jnp.float32)
            nxt = lax.rem(f + 1, 3)
            acc[nxt] = acc[nxt] + later[:, :channels]
            acc[lax.rem(f + 2, 3)] = later[:, channels:]

        return carry

    lax.fori_loop(0, frames, frame, 0)

    for j in range(2):
        co_local(j).wait()
        co_copy(j).wait_send()
        remote(actb.at[j, pl.ds(0, 2), own_cols(hi), :], cout.at[j, :, out_cols(1 - hi), :], co_send.at[j], co_sem.at[j, 1 - hi], at(seg, k, 1 - hi)).wait_recv()

    def vo_recv(j, h):
        remote(outb.at[0, pl.ds(0, 2), own_cols(hi), :], vout.at[j, :, out_cols(h), :], vo_send.at[0, 0], vo_sem.at[j, h], at(seg, k, 1 - hi)).wait_recv()

    @pl.when(seg < last)
    def _():
        for j in range(per):
            vo_recv(j, 0)
            vo_recv(j, 1)

        def sent(f, carry):
            pipe_own(f).wait_send()
            pl.when(jnp.logical_not(top))(lambda: pipe_up(f).wait_send())
            pl.when(jnp.logical_not(bottom))(lambda: pipe_down(f).wait_send())
            return carry

        lax.fori_loop(0, frames, sent, 0)

    @pl.when(seg == last)
    def _():
        for f in range(frames):
            if f // per < last:
                vo_copy(f, 0).wait_send()
                vo_copy(f, 1).wait_send()
            else:
                vo_copy(f, 1 - hi).wait_send()
                vo_local(f).wait()
                vo_recv(f % per, 1 - hi)

    send_cache_slab().wait_send()

    @pl.when(inner)
    def _():
        send_cache_edge(0).wait_send()
        send_cache_edge(1).wait_send()

    @pl.when(seg == 2)
    def _():
        for f in range(frames):
            send_slab(f).wait_send()

    @pl.when(jnp.logical_and(jnp.logical_or(seg == 1, seg == 3), inner))
    def _():
        for f in range(frames):
            send_edge(f).wait_send()


def local(video_in, cache_in, conv_weight, conv_bias, norm_gain):
    frames, held, columns, channels = video_in.shape
    rows = 2 * held + 2
    tall = rows - 2
    size = tall * PITCH
    span = rows * PITCH
    weight = conv_weight.reshape(3, 9 * channels, channels)
    cache = cache_in[0]
    per = frames // lax.axis_size("segment")
    dma = pltpu.SemaphoreType.DMA
    video_out, cache_out = pl.pallas_call(
        kernel,
        out_shape=(
            jax.ShapeDtypeStruct((per, held, columns, channels), jnp.bfloat16),
            jax.ShapeDtypeStruct(cache.shape, jnp.bfloat16),
        ),
        in_specs=[pl.BlockSpec(memory_space=pl.ANY)] * 3 + [pl.BlockSpec(memory_space=pltpu.VMEM)] * 2,
        out_specs=(pl.BlockSpec(memory_space=pl.ANY), pl.BlockSpec(memory_space=pl.ANY)),
        scratch_shapes=[
            pltpu.VMEM((9 * channels, 3 * channels), jnp.bfloat16),
            pltpu.VMEM((frames, rows, PITCH, channels), jnp.bfloat16),
            pltpu.VMEM((2, rows, PITCH, channels), jnp.bfloat16),
            pltpu.VMEM((size, 9 * channels), jnp.bfloat16),
            pltpu.VMEM((span + 16, channels), jnp.float32),
            pltpu.VMEM((3, size, channels), jnp.float32),
            pltpu.VMEM((frames, tall, PITCH, channels), jnp.bfloat16),
            pltpu.VMEM((2, tall, PITCH, channels), jnp.bfloat16),
            dma((3, 3)), dma((frames,)), dma((frames, 3)), dma((1,)), dma((frames, 3)), dma((frames,)),
            dma, dma((3,)), dma((3,)), dma((frames, 2)), dma((per, 2)), dma((2,)), dma((2, 2)),
        ],
        compiler_params=pltpu.CompilerParams(collective_id=0, has_side_effects=True, vmem_limit_bytes=60 * 2**20),
    )(video_in, cache, weight, conv_bias, norm_gain)
    return video_out, cache_out[None]


def solution(mesh):
    return jax.shard_map(
        local,
        mesh=mesh,
        in_specs=(
            P(None, "slab", None, None),
            P("segment", None, "slab", None, None),
            P("segment", None, None, None, None, None),
            P("segment", None),
            P("segment", None),
        ),
        out_specs=(P("segment", "slab", None, None), P("segment", None, "slab", None, None)),
        check_vma=False,
    )
```

```python
import jax
import jax.numpy as jnp
from jax import lax
from jax.experimental import pallas as pl
from jax.experimental.pallas import tpu as pltpu
from jax.sharding import PartitionSpec as P

MESH = pl.DeviceIdType.MESH
PAD = 8
ORDER = (1, 0, 2)


def kernel(video, cache, weight, bias, gain, vout, cout, wbuf, xin, cin, lhs, flat, acc, outb, actb,
           w_sem, loc_sem, in_sem, pipe_send, vin_send, cin_loc, cin_sem, cin_send, vo_send, vo_sem, co_sem):
    frames, held, columns, channels = video.shape
    pitch = columns + PAD
    size = held * columns
    block = 3 * channels
    seg = lax.axis_index("segment")
    slab = lax.axis_index("slab")
    last = lax.axis_size("segment") - 1
    per = frames // (last + 1)
    has_up = jnp.logical_not(slab == 0)
    has_down = jnp.logical_not(slab == lax.axis_size("slab") - 1)
    other = (last - seg, slab)
    first_seg = seg == 0
    above = lax.rem(slab + lax.axis_size("slab") - 1, lax.axis_size("slab"))
    below = lax.rem(slab + 1, lax.axis_size("slab"))
    before = lax.rem(seg + last, last + 1)
    after = lax.rem(seg + 1, last + 1)

    def remote(src, dst, send, recv, dev):
        return pltpu.make_async_remote_copy(src_ref=src, dst_ref=dst, send_sem=send, recv_sem=recv, device_id=dev, device_id_type=MESH)

    def w_copy(a, b):
        return pltpu.make_async_copy(
            weight.at[a, pl.ds(b * block, block), :],
            wbuf.at[pl.ds(ORDER.index(b) * block, block), pl.ds((2 - a) * channels, channels)],
            w_sem.at[a, b])

    def own_video(f):
        return pltpu.make_async_copy(video.at[f], xin.at[f, pl.ds(1, held)], loc_sem.at[f])

    own_cache = pltpu.make_async_copy(cache, cin.at[:, pl.ds(1, held)], cin_loc)

    @pl.when(first_seg)
    def _():
        own_video(0).start()

    w_copy(2, 1).start()
    w_copy(2, 0).start()
    w_copy(2, 2).start()
    own_cache.start()

    @pl.when(first_seg)
    def _():
        for f in range(1, frames):
            own_video(f).start()

    for a in (1, 0):
        for b in ORDER:
            w_copy(a, b).start()

    barrier = pltpu.get_barrier_semaphore()

    def greet(s, q):
        pl.semaphore_signal(barrier, inc=1, device_id=(s, q), device_id_type=MESH)

    later_seg = seg > 0
    early_seg = seg < last
    pl.when(has_up)(lambda: greet(seg, above))
    pl.when(has_down)(lambda: greet(seg, below))

    @pl.when(later_seg)
    def _():
        greet(before, slab)
        pl.when(has_up)(lambda: greet(before, above))
        pl.when(has_down)(lambda: greet(before, below))

    @pl.when(first_seg)
    def _():
        pl.when(has_up)(lambda: greet(2, above))
        pl.when(has_down)(lambda: greet(3, below))

    @pl.when(early_seg)
    def _():
        greet(last, slab)

    flat[...] = jnp.zeros_like(flat)
    acc[...] = jnp.zeros_like(acc)

    @pl.when(jnp.logical_not(has_up))
    def _():
        xin[:, 0] = jnp.zeros_like(xin[:, 0])
        cin[:, 0] = jnp.zeros_like(cin[:, 0])

    @pl.when(jnp.logical_not(has_down))
    def _():
        xin[:, held + 1] = jnp.zeros_like(xin[:, held + 1])
        cin[:, held + 1] = jnp.zeros_like(cin[:, held + 1])

    one = jnp.int32(1)
    zero = jnp.int32(0)
    ups = jnp.where(has_up, one, zero)
    downs = jnp.where(has_down, one, zero)
    expected = ups + downs
    expected += jnp.where(early_seg, 1 + ups + downs, zero)
    expected += jnp.where(seg == 2, downs, zero)
    expected += jnp.where(seg == last, ups + last, zero)
    pl.semaphore_wait(barrier, expected)

    sends_down = jnp.logical_and(seg == 2, has_down)
    sends_up = jnp.logical_and(seg == 3, has_up)

    def vin_down(f):
        return remote(video.at[f, held - 1], xin.at[f, 0], vin_send.at[f], in_sem.at[f, 1], (0, below))

    def vin_up(f):
        return remote(video.at[f, 0], xin.at[f, held + 1], vin_send.at[f], in_sem.at[f, 2], (0, above))

    def cache_down():
        return remote(cache.at[:, held - 1], cin.at[:, 0], cin_send.at[0], cin_sem.at[0], (seg, below))

    def cache_up():
        return remote(cache.at[:, 0], cin.at[:, held + 1], cin_send.at[1], cin_sem.at[1], (seg, above))

    @pl.when(sends_down)
    def _():
        for f in range(frames):
            vin_down(f).start()

    @pl.when(sends_up)
    def _():
        for f in range(frames):
            vin_up(f).start()

    def send_cache():
        pl.when(has_down)(lambda: cache_down().start())
        pl.when(has_up)(lambda: cache_up().start())

    pl.when(first_seg)(send_cache)

    gains = gain[0:1, :]
    biases = bias[0:1, :]

    def put(r, values):
        flat[r * pitch + PAD:(r + 1) * pitch] = values

    def copy_taps(b, r):
        for c in range(3):
            start = (r + b) * pitch + PAD + c - 1
            at = ORDER.index(b) * block + c * channels
            lhs[r * columns:(r + 1) * columns, at:at + channels] = flat[start:start + columns].astype(jnp.bfloat16)

    inner_taps = [(b, r) for b in ORDER for r in range(held) if 1 <= r + b <= held]
    outer_taps = [(b, r) for b in ORDER for r in range(held) if not 1 <= r + b <= held]

    def activate(values):
        values = values.astype(jnp.float32)
        mean = jnp.sum(values * values, axis=-1, keepdims=True) * (1.0 / channels)
        scaled = values * lax.rsqrt(mean + 1e-06) * gains
        return scaled / (1.0 + jnp.exp(-scaled))

    def cached_frames():
        own_cache.wait()
        pl.when(has_up)(lambda: remote(cache.at[:, 0], cin.at[:, 0], cin_send.at[0], cin_sem.at[0], other).wait_recv())
        pl.when(has_down)(lambda: remote(cache.at[:, 0], cin.at[:, held + 1], cin_send.at[1], cin_sem.at[1], other).wait_recv())

        def load(j):
            for r in range(held + 2):
                put(r, cin[j, r].astype(jnp.float32))
            for b, r in inner_taps + outer_taps:
                copy_taps(b, r)

        load(1)
        later = jnp.dot(lhs[...], wbuf[:, channels:], preferred_element_type=jnp.float32)
        acc[0] += later[:, :channels]
        acc[1] += later[:, channels:]
        load(0)
        acc[0] += jnp.dot(lhs[...], wbuf[:, 2 * channels:], preferred_element_type=jnp.float32)

    def wait_weights(a):
        for b in ORDER:
            w_copy(a, b).wait()

    @pl.when(later_seg)
    def _():
        wait_weights(2)
        wait_weights(1)
        wait_weights(0)
        send_cache()
        cached_frames()

    def pipe_own(f):
        return remote(outb.at[f], xin.at[f, pl.ds(1, held)], pipe_send.at[f, 0], in_sem.at[f, 0], (after, slab))

    def pipe_up(f):
        return remote(outb.at[f, 0], xin.at[f, held + 1], pipe_send.at[f, 1], in_sem.at[f, 2], (after, above))

    def pipe_down(f):
        return remote(outb.at[f, held - 1], xin.at[f, 0], pipe_send.at[f, 2], in_sem.at[f, 1], (after, below))

    def vo_copy(f):
        return remote(outb.at[f], vout.at[f % per], vo_send.at[f], vo_sem.at[f % per], (f // per, slab))

    def vo_local(f):
        return pltpu.make_async_copy(outb.at[f], vout.at[f % per], vo_sem.at[f % per])

    def co_local(j):
        return pltpu.make_async_copy(actb.at[j], cout.at[j], co_sem.at[j])

    def frame(f, carry):
        now = lax.rem(f, 3)

        @pl.when(first_seg)
        def _():
            own_video(f).wait()

        @pl.when(later_seg)
        def _():
            remote(outb.at[f], xin.at[f, pl.ds(1, held)], vin_send.at[f], in_sem.at[f, 0], other).wait_recv()

        for r in range(1, 1 + held):
            acts = activate(xin[f, r])
            put(r, acts)

        for b, r in inner_taps:
            copy_taps(b, r)

        @pl.when(f >= frames - 2)
        def _():
            j = f - (frames - 2)
            for r in range(held):
                actb[j, r] = flat[(r + 1) * pitch + PAD:(r + 2) * pitch].astype(jnp.bfloat16)
            co_local(j).start()

        @pl.when(jnp.logical_and(first_seg, f == 0))
        def _():
            wait_weights(2)

        acc[now] += jnp.dot(lhs[:, :block], wbuf[:block, :channels], preferred_element_type=jnp.float32)

        pl.when(has_up)(lambda: remote(outb.at[f, 0], xin.at[f, 0], vin_send.at[f], in_sem.at[f, 1], other).wait_recv())
        pl.when(has_down)(lambda: remote(outb.at[f, 0], xin.at[f, held + 1], vin_send.at[f], in_sem.at[f, 2], other).wait_recv())

        for r in (0, held + 1):
            put(r, activate(xin[f, r]))
        for b, r in outer_taps:
            copy_taps(b, r)

        conv = jnp.dot(lhs[:, block:], wbuf[block:, :channels], preferred_element_type=jnp.float32) + acc[now] + biases

        @pl.when(jnp.logical_and(first_seg, f == 0))
        def _():
            wait_weights(1)
            wait_weights(0)
            acc[0] = conv
            cached_keep = lhs[...]
            cached_frames()
            lhs[...] = cached_keep
            outb[f] = (xin[f, 1:1 + held].astype(jnp.float32).reshape(size, channels) + acc[0]).reshape(held, columns, channels).astype(jnp.bfloat16)

        @pl.when(jnp.logical_not(jnp.logical_and(first_seg, f == 0)))
        def _():
            outb[f] = (xin[f, 1:1 + held].astype(jnp.float32).reshape(size, channels) + conv).reshape(held, columns, channels).astype(jnp.bfloat16)

        @pl.when(early_seg)
        def _():
            pl.when(has_up)(lambda: pipe_up(f).start())
            pl.when(has_down)(lambda: pipe_down(f).start())
            pipe_own(f).start()

        @pl.when(seg == last)
        def _():
            pl.when(f // per < last)(lambda: vo_copy(f).start())
            pl.when(f // per == last)(lambda: vo_local(f).start())

        @pl.when(f < frames - 1)
        def _():
            later = jnp.dot(lhs[...], wbuf[:, channels:], preferred_element_type=jnp.float32)
            acc[lax.rem(f + 1, 3)] += later[:, :channels]
            acc[lax.rem(f + 2, 3)] = later[:, channels:]

        return carry

    lax.fori_loop(0, frames, frame, 0)

    for j in range(2):
        co_local(j).wait()

    @pl.when(early_seg)
    def _():
        for j in range(per):
            remote(outb.at[0], vout.at[j], vo_send.at[0], vo_sem.at[j], other).wait_recv()

        def sent(f, carry):
            pipe_own(f).wait_send()
            pl.when(has_up)(lambda: pipe_up(f).wait_send())
            pl.when(has_down)(lambda: pipe_down(f).wait_send())
            return carry

        lax.fori_loop(0, frames, sent, 0)

    @pl.when(seg == last)
    def _():
        for f in range(frames):
            if f // per < last:
                vo_copy(f).wait_send()
            else:
                vo_local(f).wait()

    pl.when(has_down)(lambda: cache_down().wait_send())
    pl.when(has_up)(lambda: cache_up().wait_send())

    @pl.when(sends_down)
    def _():
        for f in range(frames):
            vin_down(f).wait_send()

    @pl.when(sends_up)
    def _():
        for f in range(frames):
            vin_up(f).wait_send()


def local(video_in, cache_in, conv_weight, conv_bias, norm_gain):
    frames, held, columns, channels = video_in.shape
    rows = held + 2
    size = held * columns
    weight = conv_weight.reshape(3, 9 * channels, channels)
    cache = cache_in[0]
    per = frames // lax.axis_size("segment")
    dma = pltpu.SemaphoreType.DMA
    video_out, cache_out = pl.pallas_call(
        kernel,
        out_shape=(
            jax.ShapeDtypeStruct((per, held, columns, channels), jnp.bfloat16),
            jax.ShapeDtypeStruct(cache.shape, jnp.bfloat16),
        ),
        in_specs=[pl.BlockSpec(memory_space=pl.ANY)] * 3 + [pl.BlockSpec(memory_space=pltpu.VMEM)] * 2,
        out_specs=(pl.BlockSpec(memory_space=pl.ANY), pl.BlockSpec(memory_space=pl.ANY)),
        scratch_shapes=[
            pltpu.VMEM((9 * channels, 3 * channels), jnp.bfloat16),
            pltpu.VMEM((frames, rows, columns, channels), jnp.bfloat16),
            pltpu.VMEM((2, rows, columns, channels), jnp.bfloat16),
            pltpu.VMEM((size, 9 * channels), jnp.bfloat16),
            pltpu.VMEM((rows * (columns + PAD) + 8 * PAD, channels), jnp.float32),
            pltpu.VMEM((3, size, channels), jnp.float32),
            pltpu.VMEM((frames, held, columns, channels), jnp.bfloat16),
            pltpu.VMEM((2, held, columns, channels), jnp.bfloat16),
            dma((3, 3)), dma((frames,)), dma((frames, 3)), dma((frames, 3)), dma((frames,)),
            dma, dma((2,)), dma((2,)), dma((frames,)), dma((per,)), dma((2,)),
        ],
        compiler_params=pltpu.CompilerParams(collective_id=0, has_side_effects=True, vmem_limit_bytes=60 * 2**20),
    )(video_in, cache, weight, conv_bias, norm_gain)
    return video_out, cache_out[None]


def solution(mesh):
    return jax.shard_map(
        local,
        mesh=mesh,
        in_specs=(
            P(None, "slab", None, None),
            P("segment", None, "slab", None, None),
            P("segment", None, None, None, None, None),
            P("segment", None),
            P("segment", None),
        ),
        out_specs=(P("segment", "slab", None, None), P("segment", None, "slab", None, None)),
        check_vma=False,
    )
```

```python
import jax
import jax.numpy as jnp
from jax import lax
from jax.experimental import pallas as pl
from jax.experimental.pallas import tpu as pltpu
from jax.sharding import PartitionSpec as P

MESH = pl.DeviceIdType.MESH
PAD = 8
ORDER = (1, 0, 2)
EARLY = 2


def kernel(video, cache, weight, bias, gain, out, wbuf, xin, cin, lhs, flat, acc, outb, actb,
           w_sem, loc_sem, in_sem, pipe_send, vin_send, cin_loc, cin_sem, cin_send, vo_send, vo_sem, co_sem):
    frames, held, columns, channels = video.shape
    pitch = columns + PAD
    size = held * columns
    block = 3 * channels
    seg = lax.axis_index("segment")
    slab = lax.axis_index("slab")
    last = lax.axis_size("segment") - 1
    per = frames // (last + 1)
    has_up = jnp.logical_not(slab == 0)
    has_down = jnp.logical_not(slab == lax.axis_size("slab") - 1)
    other = (last - seg, slab)
    first_seg = seg == 0
    vout = out.at[0]
    cout = out.at[1]
    above = lax.rem(slab + lax.axis_size("slab") - 1, lax.axis_size("slab"))
    below = lax.rem(slab + 1, lax.axis_size("slab"))
    before = lax.rem(seg + last, last + 1)
    after = lax.rem(seg + 1, last + 1)

    def remote(src, dst, send, recv, dev):
        return pltpu.make_async_remote_copy(src_ref=src, dst_ref=dst, send_sem=send, recv_sem=recv, device_id=dev, device_id_type=MESH)

    def w_copy(a, b):
        return pltpu.make_async_copy(
            weight.at[a, pl.ds(b * block, block), :],
            wbuf.at[pl.ds(ORDER.index(b) * block, block), pl.ds((2 - a) * channels, channels)],
            w_sem.at[a, b])

    def own_video(f):
        return pltpu.make_async_copy(video.at[f], xin.at[f, pl.ds(1, held)], loc_sem.at[f])

    own_cache = pltpu.make_async_copy(cache, cin.at[:, pl.ds(1, held)], cin_loc)

    @pl.when(first_seg)
    def _():
        own_video(0).start()

    w_copy(2, 1).start()
    w_copy(2, 0).start()
    w_copy(2, 2).start()
    own_cache.start()

    @pl.when(first_seg)
    def _():
        for f in range(1, frames):
            own_video(f).start()

    for a in (1, 0):
        for b in ORDER:
            w_copy(a, b).start()

    barrier = pltpu.get_barrier_semaphore()

    def greet(s, q):
        pl.semaphore_signal(barrier, inc=1, device_id=(s, q), device_id_type=MESH)

    later_seg = seg > 0
    early_seg = seg < last
    pl.when(has_up)(lambda: greet(seg, above))
    pl.when(has_down)(lambda: greet(seg, below))

    @pl.when(later_seg)
    def _():
        greet(before, slab)
        pl.when(has_up)(lambda: greet(before, above))
        pl.when(has_down)(lambda: greet(before, below))

    @pl.when(first_seg)
    def _():
        pl.when(has_up)(lambda: greet(2, above))
        pl.when(has_down)(lambda: greet(3, below))

    @pl.when(early_seg)
    def _():
        greet(last, slab)

    flat[...] = jnp.zeros_like(flat)
    acc[...] = jnp.zeros_like(acc)

    @pl.when(jnp.logical_not(has_up))
    def _():
        xin[:, 0] = jnp.zeros_like(xin[:, 0])
        cin[:, 0] = jnp.zeros_like(cin[:, 0])

    @pl.when(jnp.logical_not(has_down))
    def _():
        xin[:, held + 1] = jnp.zeros_like(xin[:, held + 1])
        cin[:, held + 1] = jnp.zeros_like(cin[:, held + 1])

    one = jnp.int32(1)
    zero = jnp.int32(0)
    ups = jnp.where(has_up, one, zero)
    downs = jnp.where(has_down, one, zero)
    expected = ups + downs
    expected += jnp.where(early_seg, 1 + ups + downs, zero)
    expected += jnp.where(seg == 2, downs, zero)
    expected += jnp.where(seg == last, ups + last, zero)
    pl.semaphore_wait(barrier, expected)

    sends_down = jnp.logical_and(seg == 2, has_down)
    sends_up = jnp.logical_and(seg == 3, has_up)

    def vin_down(f):
        return remote(video.at[f, held - 1], xin.at[f, 0], vin_send.at[f], in_sem.at[f, 1], (0, below))

    def vin_up(f):
        return remote(video.at[f, 0], xin.at[f, held + 1], vin_send.at[f], in_sem.at[f, 2], (0, above))

    def cache_down():
        return remote(cache.at[:, held - 1], cin.at[:, 0], cin_send.at[0], cin_sem.at[0], (seg, below))

    def cache_up():
        return remote(cache.at[:, 0], cin.at[:, held + 1], cin_send.at[1], cin_sem.at[1], (seg, above))

    @pl.when(sends_down)
    def _():
        for f in range(EARLY):
            vin_down(f).start()

    @pl.when(sends_up)
    def _():
        for f in range(EARLY):
            vin_up(f).start()

    def send_cache():
        pl.when(has_down)(lambda: cache_down().start())
        pl.when(has_up)(lambda: cache_up().start())

    pl.when(first_seg)(send_cache)

    def send_edges(start, stop):
        @pl.when(sends_down)
        def _():
            for f in range(start, stop):
                vin_down(f).start()

        @pl.when(sends_up)
        def _():
            for f in range(start, stop):
                vin_up(f).start()

    gains = gain[0:1, :]
    biases = bias[0:1, :]

    def put(r, values):
        flat[r * pitch + PAD:(r + 1) * pitch] = values

    def copy_taps(b, r):
        for c in range(3):
            start = (r + b) * pitch + PAD + c - 1
            at = ORDER.index(b) * block + c * channels
            lhs[r * columns:(r + 1) * columns, at:at + channels] = flat[start:start + columns].astype(jnp.bfloat16)

    inner_taps = [(b, r) for b in ORDER for r in range(held) if 1 <= r + b <= held]
    outer_taps = [(b, r) for b in ORDER for r in range(held) if not 1 <= r + b <= held]

    def activate(values):
        values = values.astype(jnp.float32)
        mean = jnp.sum(values * values, axis=-1, keepdims=True) * (1.0 / channels)
        scaled = values * lax.rsqrt(mean + 1e-06) * gains
        return scaled / (1.0 + jnp.exp(-scaled))

    def cached_frames():
        own_cache.wait()
        pl.when(has_up)(lambda: remote(cache.at[:, 0], cin.at[:, 0], cin_send.at[0], cin_sem.at[0], other).wait_recv())
        pl.when(has_down)(lambda: remote(cache.at[:, 0], cin.at[:, held + 1], cin_send.at[1], cin_sem.at[1], other).wait_recv())

        def load(j):
            for r in range(held + 2):
                put(r, cin[j, r].astype(jnp.float32))
            for b, r in inner_taps + outer_taps:
                copy_taps(b, r)

        load(1)
        later = jnp.dot(lhs[...], wbuf[:, channels:], preferred_element_type=jnp.float32)
        acc[0] += later[:, :channels]
        acc[1] += later[:, channels:]
        load(0)
        acc[0] += jnp.dot(lhs[...], wbuf[:, 2 * channels:], preferred_element_type=jnp.float32)

    def wait_weights(a):
        for b in ORDER:
            w_copy(a, b).wait()

    @pl.when(later_seg)
    def _():
        wait_weights(2)
        wait_weights(1)
        wait_weights(0)
        send_edges(EARLY, 2 * EARLY)
        send_cache()
        cached_frames()
        send_edges(2 * EARLY, frames)

    def pipe_own(f):
        return remote(outb.at[f], xin.at[f, pl.ds(1, held)], pipe_send.at[f, 0], in_sem.at[f, 0], (after, slab))

    def pipe_up(f):
        return remote(outb.at[f, 0], xin.at[f, held + 1], pipe_send.at[f, 1], in_sem.at[f, 2], (after, above))

    def pipe_down(f):
        return remote(outb.at[f, held - 1], xin.at[f, 0], pipe_send.at[f, 2], in_sem.at[f, 1], (after, below))

    def vo_copy(f):
        return remote(outb.at[f], vout.at[f % per], vo_send.at[f], vo_sem.at[f % per], (f // per, slab))

    def vo_local(f):
        return pltpu.make_async_copy(outb.at[f], vout.at[f % per], vo_sem.at[f % per])

    def co_local(j):
        return pltpu.make_async_copy(actb.at[j], cout.at[j], co_sem.at[j])

    def frame(f, carry):
        now = lax.rem(f, 3)

        @pl.when(first_seg)
        def _():
            own_video(f).wait()

        @pl.when(later_seg)
        def _():
            remote(outb.at[f], xin.at[f, pl.ds(1, held)], vin_send.at[f], in_sem.at[f, 0], other).wait_recv()

        for r in range(1, 1 + held):
            acts = activate(xin[f, r])
            put(r, acts)

        for b, r in inner_taps:
            copy_taps(b, r)

        @pl.when(f >= frames - 2)
        def _():
            j = f - (frames - 2)
            for r in range(held):
                actb[j, r] = flat[(r + 1) * pitch + PAD:(r + 2) * pitch].astype(jnp.bfloat16)
            co_local(j).start()

        @pl.when(jnp.logical_and(first_seg, f == 0))
        def _():
            wait_weights(2)

        acc[now] += jnp.dot(lhs[:, :block], wbuf[:block, :channels], preferred_element_type=jnp.float32)

        pl.when(has_up)(lambda: remote(outb.at[f, 0], xin.at[f, 0], vin_send.at[f], in_sem.at[f, 1], other).wait_recv())
        pl.when(has_down)(lambda: remote(outb.at[f, 0], xin.at[f, held + 1], vin_send.at[f], in_sem.at[f, 2], other).wait_recv())

        for r in (0, held + 1):
            put(r, activate(xin[f, r]))
        for b, r in outer_taps:
            copy_taps(b, r)

        conv = jnp.dot(lhs[:, block:], wbuf[block:, :channels], preferred_element_type=jnp.float32) + acc[now] + biases

        @pl.when(jnp.logical_and(first_seg, f == 0))
        def _():
            wait_weights(1)
            wait_weights(0)
            acc[0] = conv
            cached_keep = lhs[...]
            cached_frames()
            lhs[...] = cached_keep
            outb[f] = (xin[f, 1:1 + held].astype(jnp.float32).reshape(size, channels) + acc[0]).reshape(held, columns, channels).astype(jnp.bfloat16)

        @pl.when(jnp.logical_not(jnp.logical_and(first_seg, f == 0)))
        def _():
            outb[f] = (xin[f, 1:1 + held].astype(jnp.float32).reshape(size, channels) + conv).reshape(held, columns, channels).astype(jnp.bfloat16)

        @pl.when(early_seg)
        def _():
            pl.when(has_up)(lambda: pipe_up(f).start())
            pl.when(has_down)(lambda: pipe_down(f).start())
            pipe_own(f).start()

        @pl.when(seg == last)
        def _():
            pl.when(f // per < last)(lambda: vo_copy(f).start())
            pl.when(f // per == last)(lambda: vo_local(f).start())

        @pl.when(f < frames - 1)
        def _():
            later = jnp.dot(lhs[...], wbuf[:, channels:], preferred_element_type=jnp.float32)
            acc[lax.rem(f + 1, 3)] += later[:, :channels]
            acc[lax.rem(f + 2, 3)] = later[:, channels:]

        return carry

    lax.fori_loop(0, frames, frame, 0)

    for j in range(2):
        co_local(j).wait()

    @pl.when(early_seg)
    def _():
        for j in range(per):
            remote(outb.at[0], vout.at[j], vo_send.at[0], vo_sem.at[j], other).wait_recv()

        def sent(f, carry):
            pipe_own(f).wait_send()
            pl.when(has_up)(lambda: pipe_up(f).wait_send())
            pl.when(has_down)(lambda: pipe_down(f).wait_send())
            return carry

        lax.fori_loop(0, frames, sent, 0)

    @pl.when(seg == last)
    def _():
        for f in range(frames):
            if f // per < last:
                vo_copy(f).wait_send()
            else:
                vo_local(f).wait()

    pl.when(has_down)(lambda: cache_down().wait_send())
    pl.when(has_up)(lambda: cache_up().wait_send())

    @pl.when(sends_down)
    def _():
        for f in range(frames):
            vin_down(f).wait_send()

    @pl.when(sends_up)
    def _():
        for f in range(frames):
            vin_up(f).wait_send()


def local(video_in, cache_in, conv_weight, conv_bias, norm_gain):
    frames, held, columns, channels = video_in.shape
    rows = held + 2
    size = held * columns
    weight = conv_weight.reshape(3, 9 * channels, channels)
    cache = cache_in[0]
    per = frames // lax.axis_size("segment")
    dma = pltpu.SemaphoreType.DMA
    both = pl.pallas_call(
        kernel,
        out_shape=jax.ShapeDtypeStruct((2, per, held, columns, channels), jnp.bfloat16),
        in_specs=[pl.BlockSpec(memory_space=pl.ANY)] * 3 + [pl.BlockSpec(memory_space=pltpu.VMEM)] * 2,
        out_specs=pl.BlockSpec(memory_space=pl.ANY),
        scratch_shapes=[
            pltpu.VMEM((9 * channels, 3 * channels), jnp.bfloat16),
            pltpu.VMEM((frames, rows, columns, channels), jnp.bfloat16),
            pltpu.VMEM((2, rows, columns, channels), jnp.bfloat16),
            pltpu.VMEM((size, 9 * channels), jnp.bfloat16),
            pltpu.VMEM((rows * (columns + PAD) + 8 * PAD, channels), jnp.float32),
            pltpu.VMEM((3, size, channels), jnp.float32),
            pltpu.VMEM((frames, held, columns, channels), jnp.bfloat16),
            pltpu.VMEM((2, held, columns, channels), jnp.bfloat16),
            dma((3, 3)), dma((frames,)), dma((frames, 3)), dma((frames, 3)), dma((frames,)),
            dma, dma((2,)), dma((2,)), dma((frames,)), dma((per,)), dma((2,)),
        ],
        compiler_params=pltpu.CompilerParams(collective_id=0, has_side_effects=True, vmem_limit_bytes=60 * 2**20),
    )(video_in, cache, weight, conv_bias, norm_gain)
    return both[0], both[1][None]


def solution(mesh):
    return jax.shard_map(
        local,
        mesh=mesh,
        in_specs=(
            P(None, "slab", None, None),
            P("segment", None, "slab", None, None),
            P("segment", None, None, None, None, None),
            P("segment", None),
            P("segment", None),
        ),
        out_specs=(P("segment", "slab", None, None), P("segment", None, "slab", None, None)),
        check_vma=False,
    )
```

```python
import jax
import jax.numpy as jnp
from jax import lax
from jax.experimental import pallas as pl
from jax.experimental.pallas import tpu as pltpu
from jax.sharding import PartitionSpec as P

MESH = pl.DeviceIdType.MESH
PAD = 8
ORDER = (1, 0, 2)
EARLY = 2


def kernel(video, cache, weight, bias, gain, out, wbuf, xin, cin, lhs, flat, acc, outb, actb,
           w_sem, loc_sem, in_sem, pipe_send, vin_send, cin_loc, cin_sem, cin_send, vo_send, vo_sem, co_sem):
    frames, held, columns, channels = video.shape
    pitch = columns + PAD
    size = held * columns
    block = 3 * channels
    seg = lax.axis_index("segment")
    slab = lax.axis_index("slab")
    last = lax.axis_size("segment") - 1
    per = frames // (last + 1)
    has_up = jnp.logical_not(slab == 0)
    has_down = jnp.logical_not(slab == lax.axis_size("slab") - 1)
    other = (last - seg, slab)
    first_seg = seg == 0
    vout = out.at[0]
    cout = out.at[1]
    above = lax.rem(slab + lax.axis_size("slab") - 1, lax.axis_size("slab"))
    below = lax.rem(slab + 1, lax.axis_size("slab"))
    before = lax.rem(seg + last, last + 1)
    after = lax.rem(seg + 1, last + 1)

    def remote(src, dst, send, recv, dev):
        return pltpu.make_async_remote_copy(src_ref=src, dst_ref=dst, send_sem=send, recv_sem=recv, device_id=dev, device_id_type=MESH)

    def w_copy(a, b):
        return pltpu.make_async_copy(
            weight.at[a, pl.ds(b * block, block), :],
            wbuf.at[pl.ds(ORDER.index(b) * block, block), pl.ds((2 - a) * channels, channels)],
            w_sem.at[a, b])

    def own_video(f):
        return pltpu.make_async_copy(video.at[f], xin.at[f, pl.ds(1, held)], loc_sem.at[f])

    own_cache = pltpu.make_async_copy(cache, cin.at[:, pl.ds(1, held)], cin_loc)

    @pl.when(first_seg)
    def _():
        own_video(0).start()

    w_copy(2, 1).start()
    w_copy(2, 0).start()
    w_copy(2, 2).start()
    own_cache.start()

    @pl.when(first_seg)
    def _():
        for f in range(1, frames):
            own_video(f).start()

    for a in (1, 0):
        for b in ORDER:
            w_copy(a, b).start()

    barrier = pltpu.get_barrier_semaphore()

    def greet(s, q):
        pl.semaphore_signal(barrier, inc=1, device_id=(s, q), device_id_type=MESH)

    later_seg = seg > 0
    early_seg = seg < last
    pl.when(has_up)(lambda: greet(seg, above))
    pl.when(has_down)(lambda: greet(seg, below))

    @pl.when(later_seg)
    def _():
        greet(before, slab)
        pl.when(has_up)(lambda: greet(before, above))
        pl.when(has_down)(lambda: greet(before, below))

    @pl.when(first_seg)
    def _():
        pl.when(has_up)(lambda: greet(2, above))
        pl.when(has_down)(lambda: greet(3, below))

    @pl.when(early_seg)
    def _():
        greet(last, slab)

    flat[...] = jnp.zeros_like(flat)
    acc[...] = jnp.zeros_like(acc)

    @pl.when(jnp.logical_not(has_up))
    def _():
        xin[:, 0] = jnp.zeros_like(xin[:, 0])
        cin[:, 0] = jnp.zeros_like(cin[:, 0])

    @pl.when(jnp.logical_not(has_down))
    def _():
        xin[:, held + 1] = jnp.zeros_like(xin[:, held + 1])
        cin[:, held + 1] = jnp.zeros_like(cin[:, held + 1])

    one = jnp.int32(1)
    zero = jnp.int32(0)
    ups = jnp.where(has_up, one, zero)
    downs = jnp.where(has_down, one, zero)
    expected = ups + downs
    expected += jnp.where(early_seg, 1 + ups + downs, zero)
    expected += jnp.where(seg == 2, downs, zero)
    expected += jnp.where(seg == last, ups + last, zero)
    pl.semaphore_wait(barrier, expected)

    sends_down = jnp.logical_and(seg == 2, has_down)
    sends_up = jnp.logical_and(seg == 3, has_up)

    def vin_down(f):
        return remote(video.at[f, held - 1], xin.at[f, 0], vin_send.at[f], in_sem.at[f, 1], (0, below))

    def vin_up(f):
        return remote(video.at[f, 0], xin.at[f, held + 1], vin_send.at[f], in_sem.at[f, 2], (0, above))

    def cache_down():
        return remote(cache.at[:, held - 1], cin.at[:, 0], cin_send.at[0], cin_sem.at[0], (seg, below))

    def cache_up():
        return remote(cache.at[:, 0], cin.at[:, held + 1], cin_send.at[1], cin_sem.at[1], (seg, above))

    @pl.when(sends_down)
    def _():
        for f in range(EARLY):
            vin_down(f).start()

    @pl.when(sends_up)
    def _():
        for f in range(EARLY):
            vin_up(f).start()

    def send_cache():
        pl.when(has_down)(lambda: cache_down().start())
        pl.when(has_up)(lambda: cache_up().start())

    pl.when(first_seg)(send_cache)

    def send_edges(start, stop):
        @pl.when(sends_down)
        def _():
            for f in range(start, stop):
                vin_down(f).start()

        @pl.when(sends_up)
        def _():
            for f in range(start, stop):
                vin_up(f).start()

    gains = gain[0:1, :]
    biases = bias[0:1, :]

    def put(r, values):
        flat[r * pitch + PAD:(r + 1) * pitch] = values

    def copy_taps(b, r):
        for c in range(3):
            start = (r + b) * pitch + PAD + c - 1
            at = ORDER.index(b) * block + c * channels
            lhs[r * columns:(r + 1) * columns, at:at + channels] = flat[start:start + columns].astype(jnp.bfloat16)

    inner_taps = [(b, r) for b in ORDER for r in range(held) if 1 <= r + b <= held]
    outer_taps = [(b, r) for b in ORDER for r in range(held) if not 1 <= r + b <= held]

    def activate(values):
        values = values.astype(jnp.float32)
        mean = jnp.sum(values * values, axis=-1, keepdims=True) * (1.0 / channels)
        scaled = values * lax.rsqrt(mean + 1e-06) * gains
        return scaled / (1.0 + jnp.exp(-scaled))

    def cached_frames():
        own_cache.wait()
        pl.when(has_up)(lambda: remote(cache.at[:, 0], cin.at[:, 0], cin_send.at[0], cin_sem.at[0], other).wait_recv())
        pl.when(has_down)(lambda: remote(cache.at[:, 0], cin.at[:, held + 1], cin_send.at[1], cin_sem.at[1], other).wait_recv())

        def load(j):
            for r in range(held + 2):
                put(r, cin[j, r].astype(jnp.float32))
            for b, r in inner_taps + outer_taps:
                copy_taps(b, r)

        load(1)
        later = jnp.dot(lhs[...], wbuf[:, channels:], preferred_element_type=jnp.float32)
        acc[0] += later[:, :channels]
        acc[1] += later[:, channels:]
        load(0)
        acc[0] += jnp.dot(lhs[...], wbuf[:, 2 * channels:], preferred_element_type=jnp.float32)

    def wait_weights(a):
        for b in ORDER:
            w_copy(a, b).wait()

    @pl.when(later_seg)
    def _():
        wait_weights(2)
        wait_weights(1)
        wait_weights(0)
        send_cache()
        send_edges(EARLY, 2 * EARLY)
        cached_frames()
        send_edges(2 * EARLY, frames)

    def pipe_own(f):
        return remote(outb.at[f], xin.at[f, pl.ds(1, held)], pipe_send.at[f, 0], in_sem.at[f, 0], (after, slab))

    def pipe_up(f):
        return remote(outb.at[f, 0], xin.at[f, held + 1], pipe_send.at[f, 1], in_sem.at[f, 2], (after, above))

    def pipe_down(f):
        return remote(outb.at[f, held - 1], xin.at[f, 0], pipe_send.at[f, 2], in_sem.at[f, 1], (after, below))

    def vo_copy(f):
        return remote(outb.at[f], vout.at[f % per], vo_send.at[f], vo_sem.at[f % per], (f // per, slab))

    def vo_local(f):
        return pltpu.make_async_copy(outb.at[f], vout.at[f % per], vo_sem.at[f % per])

    def co_local(j):
        return pltpu.make_async_copy(actb.at[j], cout.at[j], co_sem.at[j])

    def frame(f, carry):
        now = lax.rem(f, 3)

        @pl.when(first_seg)
        def _():
            own_video(f).wait()

        @pl.when(later_seg)
        def _():
            remote(outb.at[f], xin.at[f, pl.ds(1, held)], vin_send.at[f], in_sem.at[f, 0], other).wait_recv()

        for r in range(1, 1 + held):
            acts = activate(xin[f, r])
            put(r, acts)

        for b, r in inner_taps:
            copy_taps(b, r)

        @pl.when(f >= frames - 2)
        def _():
            j = f - (frames - 2)
            for r in range(held):
                actb[j, r] = flat[(r + 1) * pitch + PAD:(r + 2) * pitch].astype(jnp.bfloat16)
            co_local(j).start()

        @pl.when(jnp.logical_and(first_seg, f == 0))
        def _():
            wait_weights(2)

        acc[now] += jnp.dot(lhs[:, :block], wbuf[:block, :channels], preferred_element_type=jnp.float32)

        pl.when(has_up)(lambda: remote(outb.at[f, 0], xin.at[f, 0], vin_send.at[f], in_sem.at[f, 1], other).wait_recv())
        pl.when(has_down)(lambda: remote(outb.at[f, 0], xin.at[f, held + 1], vin_send.at[f], in_sem.at[f, 2], other).wait_recv())

        for r in (0, held + 1):
            put(r, activate(xin[f, r]))
        for b, r in outer_taps:
            copy_taps(b, r)

        conv = jnp.dot(lhs[:, block:], wbuf[block:, :channels], preferred_element_type=jnp.float32) + acc[now] + biases

        @pl.when(jnp.logical_and(first_seg, f == 0))
        def _():
            wait_weights(1)
            wait_weights(0)
            acc[0] = conv
            cached_keep = lhs[...]
            cached_frames()
            lhs[...] = cached_keep
            outb[f] = (xin[f, 1:1 + held].astype(jnp.float32).reshape(size, channels) + acc[0]).reshape(held, columns, channels).astype(jnp.bfloat16)

        @pl.when(jnp.logical_not(jnp.logical_and(first_seg, f == 0)))
        def _():
            outb[f] = (xin[f, 1:1 + held].astype(jnp.float32).reshape(size, channels) + conv).reshape(held, columns, channels).astype(jnp.bfloat16)

        @pl.when(early_seg)
        def _():
            @pl.when(slab % 2 == 0)
            def _():
                pl.when(has_up)(lambda: pipe_up(f).start())
                pipe_down(f).start()

            @pl.when(slab % 2 == 1)
            def _():
                pl.when(has_down)(lambda: pipe_down(f).start())
                pipe_up(f).start()

            pipe_own(f).start()

        @pl.when(seg == last)
        def _():
            pl.when(f // per < last)(lambda: vo_copy(f).start())
            pl.when(f // per == last)(lambda: vo_local(f).start())

        @pl.when(f < frames - 1)
        def _():
            later = jnp.dot(lhs[...], wbuf[:, channels:], preferred_element_type=jnp.float32)
            acc[lax.rem(f + 1, 3)] += later[:, :channels]
            acc[lax.rem(f + 2, 3)] = later[:, channels:]

        return carry

    lax.fori_loop(0, frames, frame, 0)

    for j in range(2):
        co_local(j).wait()

    @pl.when(early_seg)
    def _():
        for j in range(per):
            remote(outb.at[0], vout.at[j], vo_send.at[0], vo_sem.at[j], other).wait_recv()

        def sent(f, carry):
            pipe_own(f).wait_send()
            pl.when(has_up)(lambda: pipe_up(f).wait_send())
            pl.when(has_down)(lambda: pipe_down(f).wait_send())
            return carry

        lax.fori_loop(0, frames, sent, 0)

    @pl.when(seg == last)
    def _():
        for f in range(frames):
            if f // per < last:
                vo_copy(f).wait_send()
            else:
                vo_local(f).wait()

    pl.when(has_down)(lambda: cache_down().wait_send())
    pl.when(has_up)(lambda: cache_up().wait_send())

    @pl.when(sends_down)
    def _():
        for f in range(frames):
            vin_down(f).wait_send()

    @pl.when(sends_up)
    def _():
        for f in range(frames):
            vin_up(f).wait_send()


def local(video_in, cache_in, conv_weight, conv_bias, norm_gain):
    frames, held, columns, channels = video_in.shape
    rows = held + 2
    size = held * columns
    weight = conv_weight.reshape(3, 9 * channels, channels)
    cache = cache_in[0]
    per = frames // lax.axis_size("segment")
    dma = pltpu.SemaphoreType.DMA
    both = pl.pallas_call(
        kernel,
        out_shape=jax.ShapeDtypeStruct((2, per, held, columns, channels), jnp.bfloat16),
        in_specs=[pl.BlockSpec(memory_space=pl.ANY)] * 3 + [pl.BlockSpec(memory_space=pltpu.VMEM)] * 2,
        out_specs=pl.BlockSpec(memory_space=pl.ANY),
        scratch_shapes=[
            pltpu.VMEM((9 * channels, 3 * channels), jnp.bfloat16),
            pltpu.VMEM((frames, rows, columns, channels), jnp.bfloat16),
            pltpu.VMEM((2, rows, columns, channels), jnp.bfloat16),
            pltpu.VMEM((size, 9 * channels), jnp.bfloat16),
            pltpu.VMEM((rows * (columns + PAD) + 8 * PAD, channels), jnp.float32),
            pltpu.VMEM((3, size, channels), jnp.float32),
            pltpu.VMEM((frames, held, columns, channels), jnp.bfloat16),
            pltpu.VMEM((2, held, columns, channels), jnp.bfloat16),
            dma((3, 3)), dma((frames,)), dma((frames, 3)), dma((frames, 3)), dma((frames,)),
            dma, dma((2,)), dma((2,)), dma((frames,)), dma((per,)), dma((2,)),
        ],
        compiler_params=pltpu.CompilerParams(collective_id=0, has_side_effects=True, vmem_limit_bytes=60 * 2**20),
    )(video_in, cache, weight, conv_bias, norm_gain)
    return both[0], both[1][None]


def solution(mesh):
    return jax.shard_map(
        local,
        mesh=mesh,
        in_specs=(
            P(None, "slab", None, None),
            P("segment", None, "slab", None, None),
            P("segment", None, None, None, None, None),
            P("segment", None),
            P("segment", None),
        ),
        out_specs=(P("segment", "slab", None, None), P("segment", None, "slab", None, None)),
        check_vma=False,
    )
```

```python
import jax
import jax.numpy as jnp
from jax import lax
from jax.experimental import pallas as pl
from jax.experimental.pallas import tpu as pltpu
from jax.sharding import PartitionSpec as P

MESH = pl.DeviceIdType.MESH
PAD = 8
ORDER = (1, 0, 2)
EARLY = 3


def kernel(video, cache, weight, bias, gain, out, wbuf, xin, cin, lhs, flat, acc, outb, actb,
           w_sem, loc_sem, in_sem, pipe_send, vin_send, cin_loc, cin_sem, cin_send, vo_send, vo_sem, co_sem):
    frames, held, columns, channels = video.shape
    pitch = columns + PAD
    size = held * columns
    block = 3 * channels
    seg = lax.axis_index("segment")
    slab = lax.axis_index("slab")
    last = lax.axis_size("segment") - 1
    per = frames // (last + 1)
    has_up = jnp.logical_not(slab == 0)
    has_down = jnp.logical_not(slab == lax.axis_size("slab") - 1)
    other = (last - seg, slab)
    first_seg = seg == 0
    vout = out.at[0]
    cout = out.at[1]
    above = lax.rem(slab + lax.axis_size("slab") - 1, lax.axis_size("slab"))
    below = lax.rem(slab + 1, lax.axis_size("slab"))
    before = lax.rem(seg + last, last + 1)
    after = lax.rem(seg + 1, last + 1)

    def remote(src, dst, send, recv, dev):
        return pltpu.make_async_remote_copy(src_ref=src, dst_ref=dst, send_sem=send, recv_sem=recv, device_id=dev, device_id_type=MESH)

    def w_copy(a, b):
        return pltpu.make_async_copy(
            weight.at[a, pl.ds(b * block, block), :],
            wbuf.at[pl.ds(ORDER.index(b) * block, block), pl.ds((2 - a) * channels, channels)],
            w_sem.at[a, b])

    def own_video(f):
        return pltpu.make_async_copy(video.at[f], xin.at[f, pl.ds(1, held)], loc_sem.at[f])

    own_cache = pltpu.make_async_copy(cache, cin.at[:, pl.ds(1, held)], cin_loc)

    @pl.when(first_seg)
    def _():
        own_video(0).start()

    w_copy(2, 1).start()
    w_copy(2, 0).start()
    w_copy(2, 2).start()
    own_cache.start()

    @pl.when(first_seg)
    def _():
        for f in range(1, frames):
            own_video(f).start()

    for a in (1, 0):
        for b in ORDER:
            w_copy(a, b).start()

    barrier = pltpu.get_barrier_semaphore()

    def greet(s, q):
        pl.semaphore_signal(barrier, inc=1, device_id=(s, q), device_id_type=MESH)

    later_seg = seg > 0
    early_seg = seg < last
    pl.when(has_up)(lambda: greet(seg, above))
    pl.when(has_down)(lambda: greet(seg, below))

    @pl.when(later_seg)
    def _():
        greet(before, slab)
        pl.when(has_up)(lambda: greet(before, above))
        pl.when(has_down)(lambda: greet(before, below))

    @pl.when(first_seg)
    def _():
        pl.when(has_up)(lambda: greet(2, above))
        pl.when(has_down)(lambda: greet(3, below))

    @pl.when(early_seg)
    def _():
        greet(last, slab)

    flat[...] = jnp.zeros_like(flat)
    acc[...] = jnp.zeros_like(acc)

    @pl.when(jnp.logical_not(has_up))
    def _():
        xin[:, 0] = jnp.zeros_like(xin[:, 0])
        cin[:, 0] = jnp.zeros_like(cin[:, 0])

    @pl.when(jnp.logical_not(has_down))
    def _():
        xin[:, held + 1] = jnp.zeros_like(xin[:, held + 1])
        cin[:, held + 1] = jnp.zeros_like(cin[:, held + 1])

    one = jnp.int32(1)
    zero = jnp.int32(0)
    ups = jnp.where(has_up, one, zero)
    downs = jnp.where(has_down, one, zero)
    expected = ups + downs
    expected += jnp.where(early_seg, 1 + ups + downs, zero)
    expected += jnp.where(seg == 2, downs, zero)
    expected += jnp.where(seg == last, ups + last, zero)
    pl.semaphore_wait(barrier, expected)

    sends_down = jnp.logical_and(seg == 2, has_down)
    sends_up = jnp.logical_and(seg == 3, has_up)

    def vin_down(f):
        return remote(video.at[f, held - 1], xin.at[f, 0], vin_send.at[f], in_sem.at[f, 1], (0, below))

    def vin_up(f):
        return remote(video.at[f, 0], xin.at[f, held + 1], vin_send.at[f], in_sem.at[f, 2], (0, above))

    def cache_down():
        return remote(cache.at[:, held - 1], cin.at[:, 0], cin_send.at[0], cin_sem.at[0], (seg, below))

    def cache_up():
        return remote(cache.at[:, 0], cin.at[:, held + 1], cin_send.at[1], cin_sem.at[1], (seg, above))

    @pl.when(sends_down)
    def _():
        for f in range(EARLY):
            vin_down(f).start()

    @pl.when(sends_up)
    def _():
        for f in range(EARLY):
            vin_up(f).start()

    def send_cache():
        pl.when(has_down)(lambda: cache_down().start())
        pl.when(has_up)(lambda: cache_up().start())

    pl.when(first_seg)(send_cache)

    def send_edges(start, stop):
        @pl.when(sends_down)
        def _():
            for f in range(start, stop):
                vin_down(f).start()

        @pl.when(sends_up)
        def _():
            for f in range(start, stop):
                vin_up(f).start()

    gains = gain[0:1, :]
    biases = bias[0:1, :]

    def put(r, values):
        flat[r * pitch + PAD:(r + 1) * pitch] = values

    def copy_taps(b, r):
        for c in range(3):
            start = (r + b) * pitch + PAD + c - 1
            at = ORDER.index(b) * block + c * channels
            lhs[r * columns:(r + 1) * columns, at:at + channels] = flat[start:start + columns].astype(jnp.bfloat16)

    inner_taps = [(b, r) for b in ORDER for r in range(held) if 1 <= r + b <= held]
    outer_taps = [(b, r) for b in ORDER for r in range(held) if not 1 <= r + b <= held]

    def activate(values):
        values = values.astype(jnp.float32)
        mean = jnp.sum(values * values, axis=-1, keepdims=True) * (1.0 / channels)
        scaled = values * lax.rsqrt(mean + 1e-06) * gains
        return scaled / (1.0 + jnp.exp(-scaled))

    def cached_frames():
        own_cache.wait()
        pl.when(has_up)(lambda: remote(cache.at[:, 0], cin.at[:, 0], cin_send.at[0], cin_sem.at[0], other).wait_recv())
        pl.when(has_down)(lambda: remote(cache.at[:, 0], cin.at[:, held + 1], cin_send.at[1], cin_sem.at[1], other).wait_recv())

        def load(j):
            for r in range(held + 2):
                put(r, cin[j, r].astype(jnp.float32))
            for b, r in inner_taps + outer_taps:
                copy_taps(b, r)

        load(1)
        later = jnp.dot(lhs[...], wbuf[:, channels:], preferred_element_type=jnp.float32)
        acc[0] += later[:, :channels]
        acc[1] += later[:, channels:]
        load(0)
        acc[0] += jnp.dot(lhs[...], wbuf[:, 2 * channels:], preferred_element_type=jnp.float32)

    def wait_weights(a):
        for b in ORDER:
            w_copy(a, b).wait()

    @pl.when(later_seg)
    def _():
        wait_weights(2)
        wait_weights(1)
        wait_weights(0)
        send_cache()
        send_edges(EARLY, EARLY + 2)
        cached_frames()
        send_edges(EARLY + 2, frames)

    def pipe_own(f):
        return remote(outb.at[f], xin.at[f, pl.ds(1, held)], pipe_send.at[f, 0], in_sem.at[f, 0], (after, slab))

    def pipe_up(f):
        return remote(outb.at[f, 0], xin.at[f, held + 1], pipe_send.at[f, 1], in_sem.at[f, 2], (after, above))

    def pipe_down(f):
        return remote(outb.at[f, held - 1], xin.at[f, 0], pipe_send.at[f, 2], in_sem.at[f, 1], (after, below))

    def vo_copy(f):
        return remote(outb.at[f], vout.at[f % per], vo_send.at[f], vo_sem.at[f % per], (f // per, slab))

    def vo_local(f):
        return pltpu.make_async_copy(outb.at[f], vout.at[f % per], vo_sem.at[f % per])

    def co_local(j):
        return pltpu.make_async_copy(actb.at[j], cout.at[j], co_sem.at[j])

    def frame(f, carry):
        now = lax.rem(f, 3)

        @pl.when(first_seg)
        def _():
            own_video(f).wait()

        @pl.when(later_seg)
        def _():
            remote(outb.at[f], xin.at[f, pl.ds(1, held)], vin_send.at[f], in_sem.at[f, 0], other).wait_recv()

        for r in range(1, 1 + held):
            acts = activate(xin[f, r])
            put(r, acts)

        for b, r in inner_taps:
            copy_taps(b, r)

        @pl.when(f >= frames - 2)
        def _():
            j = f - (frames - 2)
            for r in range(held):
                actb[j, r] = flat[(r + 1) * pitch + PAD:(r + 2) * pitch].astype(jnp.bfloat16)
            co_local(j).start()

        @pl.when(jnp.logical_and(first_seg, f == 0))
        def _():
            wait_weights(2)

        acc[now] += jnp.dot(lhs[:, :block], wbuf[:block, :channels], preferred_element_type=jnp.float32)

        pl.when(has_up)(lambda: remote(outb.at[f, 0], xin.at[f, 0], vin_send.at[f], in_sem.at[f, 1], other).wait_recv())
        pl.when(has_down)(lambda: remote(outb.at[f, 0], xin.at[f, held + 1], vin_send.at[f], in_sem.at[f, 2], other).wait_recv())

        for r in (0, held + 1):
            put(r, activate(xin[f, r]))
        for b, r in outer_taps:
            copy_taps(b, r)

        conv = jnp.dot(lhs[:, block:], wbuf[block:, :channels], preferred_element_type=jnp.float32) + acc[now] + biases

        @pl.when(jnp.logical_and(first_seg, f == 0))
        def _():
            wait_weights(1)
            wait_weights(0)
            acc[0] = conv
            cached_keep = lhs[...]
            cached_frames()
            lhs[...] = cached_keep
            outb[f] = (xin[f, 1:1 + held].astype(jnp.float32).reshape(size, channels) + acc[0]).reshape(held, columns, channels).astype(jnp.bfloat16)

        @pl.when(jnp.logical_not(jnp.logical_and(first_seg, f == 0)))
        def _():
            outb[f] = (xin[f, 1:1 + held].astype(jnp.float32).reshape(size, channels) + conv).reshape(held, columns, channels).astype(jnp.bfloat16)

        @pl.when(early_seg)
        def _():
            @pl.when(slab % 2 == 0)
            def _():
                pl.when(has_up)(lambda: pipe_up(f).start())
                pipe_down(f).start()

            @pl.when(slab % 2 == 1)
            def _():
                pl.when(has_down)(lambda: pipe_down(f).start())
                pipe_up(f).start()

            pipe_own(f).start()

        @pl.when(seg == last)
        def _():
            pl.when(f // per < last)(lambda: vo_copy(f).start())
            pl.when(f // per == last)(lambda: vo_local(f).start())

        @pl.when(f < frames - 1)
        def _():
            later = jnp.dot(lhs[...], wbuf[:, channels:], preferred_element_type=jnp.float32)
            acc[lax.rem(f + 1, 3)] += later[:, :channels]
            acc[lax.rem(f + 2, 3)] = later[:, channels:]

        return carry

    lax.fori_loop(0, frames, frame, 0)

    for j in range(2):
        co_local(j).wait()

    @pl.when(early_seg)
    def _():
        for j in range(per):
            remote(outb.at[0], vout.at[j], vo_send.at[0], vo_sem.at[j], other).wait_recv()

        def sent(f, carry):
            pipe_own(f).wait_send()
            pl.when(has_up)(lambda: pipe_up(f).wait_send())
            pl.when(has_down)(lambda: pipe_down(f).wait_send())
            return carry

        lax.fori_loop(0, frames, sent, 0)

    @pl.when(seg == last)
    def _():
        for f in range(frames):
            if f // per < last:
                vo_copy(f).wait_send()
            else:
                vo_local(f).wait()

    pl.when(has_down)(lambda: cache_down().wait_send())
    pl.when(has_up)(lambda: cache_up().wait_send())

    @pl.when(sends_down)
    def _():
        for f in range(frames):
            vin_down(f).wait_send()

    @pl.when(sends_up)
    def _():
        for f in range(frames):
            vin_up(f).wait_send()


def local(video_in, cache_in, conv_weight, conv_bias, norm_gain):
    frames, held, columns, channels = video_in.shape
    rows = held + 2
    size = held * columns
    weight = conv_weight.reshape(3, 9 * channels, channels)
    cache = cache_in[0]
    per = frames // lax.axis_size("segment")
    dma = pltpu.SemaphoreType.DMA
    both = pl.pallas_call(
        kernel,
        out_shape=jax.ShapeDtypeStruct((2, per, held, columns, channels), jnp.bfloat16),
        in_specs=[pl.BlockSpec(memory_space=pl.ANY)] * 3 + [pl.BlockSpec(memory_space=pltpu.VMEM)] * 2,
        out_specs=pl.BlockSpec(memory_space=pl.ANY),
        scratch_shapes=[
            pltpu.VMEM((9 * channels, 3 * channels), jnp.bfloat16),
            pltpu.VMEM((frames, rows, columns, channels), jnp.bfloat16),
            pltpu.VMEM((2, rows, columns, channels), jnp.bfloat16),
            pltpu.VMEM((size, 9 * channels), jnp.bfloat16),
            pltpu.VMEM((rows * (columns + PAD) + 8 * PAD, channels), jnp.float32),
            pltpu.VMEM((3, size, channels), jnp.float32),
            pltpu.VMEM((frames, held, columns, channels), jnp.bfloat16),
            pltpu.VMEM((2, held, columns, channels), jnp.bfloat16),
            dma((3, 3)), dma((frames,)), dma((frames, 3)), dma((frames, 3)), dma((frames,)),
            dma, dma((2,)), dma((2,)), dma((frames,)), dma((per,)), dma((2,)),
        ],
        compiler_params=pltpu.CompilerParams(collective_id=0, has_side_effects=True, vmem_limit_bytes=60 * 2**20),
    )(video_in, cache, weight, conv_bias, norm_gain)
    return both[0], both[1][None]


def solution(mesh):
    return jax.shard_map(
        local,
        mesh=mesh,
        in_specs=(
            P(None, "slab", None, None),
            P("segment", None, "slab", None, None),
            P("segment", None, None, None, None, None),
            P("segment", None),
            P("segment", None),
        ),
        out_specs=(P("segment", "slab", None, None), P("segment", None, "slab", None, None)),
        check_vma=False,
    )
```
